32 devices in a mesh: section: 2 (over y), dp: 16 (over z, x, core).
Axes of the slice: x: 2, y: 2, z: 4, core: 2. Of those that a mesh axis runs over, the one named last changes fastest.
Arguments:
- page_fine: bfloat16 [32, 1024, 256], P('dp', None, 'section'), as said below
- page_coarse: bfloat16 [32, 256, 256], P('dp', None, 'section'), as said below
- interp_fine: bfloat16 [16384, 1024], P('dp'), as said below
- interp_coarse: bfloat16 [16384, 256], P('dp'), as said below
- region_page: int32 [16384], P('dp'), may hold values from 0 to 31, as said below
- region_count: int32 [32], P('dp'), may hold values from 170 to 512, as said below
- projection: bfloat16 [256, 768], P('section'), may hold values from -0.375 to 0.375
- bn_gain: float32 [768], replicated, may hold values from 0.5 to 1.5
- bn_bias: float32 [768], replicated, may hold values from -1 to 1
- attn_in: bfloat16 [2, 3, 768, 768], P('section'), may hold values from -0.3125 to 0.3125
- attn_bias: float32 [2, 2, 768], P('section'), may hold values from -3 to 3
- attn_out: bfloat16 [2, 768, 768], P('section'), may hold values from -0.875 to 0.875
- attn_out_bias: float32 [2, 768], P('section'), may hold values from -3 to 3
- ln_gain: float32 [2, 2, 768], P('section'), may hold values from 0.5 to 1.5
- ln_bias: float32 [2, 2, 768], P('section'), may hold values from -0.5 to 0.5
- w_up: bfloat16 [2, 768, 3072], P('section'), may hold values from -0.21875 to 0.21875
- b_up: float32 [2, 3072], P('section'), may hold values from -3 to 3
- w_down: bfloat16 [2, 3072, 768], P('section'), may hold values from -0.109375 to 0.109375
- b_down: float32 [2, 768], P('section'), may hold values from -3 to 3
- cotangent: bfloat16 [16384, 768], P('dp'), may hold values from -6 to 6
Outputs:
- layer_rows: bfloat16 [2, 16384, 768], P('section', 'dp')
- fine_grad: float32 [32, 1024, 256], P('dp', None, 'section')
- coarse_grad: float32 [32, 256, 256], P('dp', None, 'section')
- proj_grad: float32 [256, 768], P('section')
- bn_gain_grad: float32 [768], replicated
- bn_bias_grad: float32 [768], replicated
- bn_mean: float32 [768], replicated
- bn_var: float32 [768], replicated
- attn_in_grad: float32 [2, 3, 768, 768], P('section')
- attn_bias_grad: float32 [2, 2, 768], P('section')
- attn_out_grad: float32 [2, 768, 768], P('section')
- attn_out_bias_grad: float32 [2, 768], P('section')
- ln_gain_grad: float32 [2, 2, 768], P('section')
- ln_bias_grad: float32 [2, 2, 768], P('section')
- w_up_grad: float32 [2, 768, 3072], P('section')
- b_up_grad: float32 [2, 3072], P('section')
- w_down_grad: float32 [2, 3072, 768], P('section')
- b_down_grad: float32 [2, 768], P('section')
The draws below stay inside these ranges and needn't reach their ends.
Inputs may be any that keep to these rules, and one draw needn't show every extreme that they name: `region_page`: rows 1024 b to 1024 b + 1023 name only pages 2 b to 2 b + 1. `region_count`: the live regions of a sequence are its first slots; the other slots are padding. `interp_fine`: nonnegative; each row sums to one before rounding. `interp_coarse`: nonnegative; each row sums to one before rounding. `page_fine`: nonnegative. `page_coarse`: nonnegative.
All inputs are finite; a program needn't handle non-finite values.
Results may differ from the reference program's by a relative error of at most 0.02.
The reference program's roundings to bfloat16 on the way (of `pooled`, `first_in`, `mixed` and `active`) count: a program that leaves them out, or rounds other values in their place, can miss the bound.
Values may be sent and summed in bfloat16 or wider, within the bound.
No kernel may reach another device: no remote copies, remote signals or barrier semaphores. Data moves between devices by JAX's collectives and lax.ppermute only.
A program may use at most 256 MiB of HBM per device.

```python
import math
import jax
import jax.numpy as jnp
from jax import lax

D = 768
HEADS = 12
HEAD = 64
FF = 3072
C = 256
FINE_SIDE = 32
COARSE_SIDE = 16
PAGES_DEV = 2
SEQ = 512
PIX1 = 1024
PIX2 = 256
TOK_DEV = 1024
TOKENS = 16384
NSEQ = 32
PAGES = 32
N_DP = 16


def draw_region_page(key, part):
    row_ids = jnp.arange(TOKENS, dtype=jnp.int32)
    within = row_ids % TOK_DEV
    picked = jax.random.randint(key, (TOKENS,), 0, PAGES_DEV, dtype=jnp.int32)
    picked = jnp.where(within == 0, 0, jnp.where(within == TOK_DEV - 1, PAGES_DEV - 1, picked))
    return row_ids // TOK_DEV * PAGES_DEV + picked


def draw_region_count(key, part):
    order = jnp.arange(NSEQ, dtype=jnp.int32)
    lowest = SEQ // 3
    base = lowest + (SEQ - lowest) * order // max(NSEQ - 1, 1)
    jitter = jax.random.randint(key, (NSEQ,), 0, max(SEQ // 4, 3), dtype=jnp.int32)
    counts = jnp.maximum(base - jitter, lowest)
    return jnp.where(order == NSEQ - 1, SEQ, counts).astype(jnp.int32)


def page_scale():
    return 10.0 ** (jnp.arange(PAGES, dtype=jnp.float32) / max(PAGES - 1, 1))


def drawn_maps(key, pixels):
    values = jnp.abs(jax.random.normal(key, (PAGES, pixels, C), jnp.float32))
    return (values * page_scale()[:, None, None]).astype(jnp.bfloat16)


def draw_page_fine(key, part):
    return drawn_maps(jax.random.fold_in(key, 11), PIX1)


def draw_page_coarse(key, part):
    return drawn_maps(jax.random.fold_in(key, 13), PIX2)


def tent_weights(key, side_cells):
    pieces = jax.random.split(key, 3)
    centre_x = jax.random.uniform(pieces[0], (TOKENS, 1), jnp.float32, 0.0, side_cells - 1.0)
    centre_y = jax.random.uniform(pieces[1], (TOKENS, 1), jnp.float32, 0.0, side_cells - 1.0)
    reach = jax.random.uniform(pieces[2], (TOKENS, 1), jnp.float32, 0.25, side_cells / 4.0)
    cells = jnp.arange(side_cells, dtype=jnp.float32)[None, :]

    def axis_weights(centre):
        lower = jnp.clip(centre - 0.5 * reach, 0.0, side_cells - 1.0)
        upper = jnp.clip(centre + 0.5 * reach, 0.0, side_cells - 1.0)
        first = jnp.maximum(0.0, 1.0 - jnp.abs(cells - lower))
        second = jnp.maximum(0.0, 1.0 - jnp.abs(cells - upper))
        return 0.5 * (first + second)
    weights = axis_weights(centre_x)[:, :, None] * axis_weights(centre_y)[:, None, :]
    return weights.reshape(TOKENS, side_cells * side_cells).astype(jnp.bfloat16)


def draw_interp_fine(key, part):
    return tent_weights(jax.random.fold_in(key, 17), FINE_SIDE)


def draw_interp_coarse(key, part):
    return tent_weights(jax.random.fold_in(key, 19), COARSE_SIDE)


def steps_of(key, dims, cuts, least, top_value):
    level, own = 1.0, jax.random.fold_in(key, 6)
    for axis_at, blocks in cuts:
        steps = jnp.exp(jax.random.uniform(jax.random.fold_in(own, axis_at), (blocks,), jnp.float32, least / len(cuts), top_value / len(cuts)))
        level = level * jnp.repeat(steps, dims[axis_at] // blocks).reshape([-1 if axis == axis_at else 1 for axis in range(len(dims))])
    return level


def bell_draw(stream_key, shape, scale, bound, cuts=(), kind=jnp.bfloat16):
    values = jax.random.normal(stream_key, shape, jnp.float32) * scale
    if len(cuts) > 0:
        values = steps_of(stream_key, shape, cuts, -0.22, 0.18) * values
    return jnp.clip(values, min=-bound, max=bound).astype(kind)


def setup_inputs(seed: int = 0) -> dict:
    key_list = jax.random.split(jax.random.key(seed), 21)
    page_fine = draw_page_fine(jax.random.fold_in(key_list[20], 71), 0)
    page_coarse = draw_page_coarse(jax.random.fold_in(key_list[20], 71), 0)
    interp_fine = draw_interp_fine(jax.random.fold_in(key_list[20], 71), 0)
    interp_coarse = draw_interp_coarse(jax.random.fold_in(key_list[20], 71), 0)
    region_page = draw_region_page(jax.random.fold_in(key_list[20], 71), 0)
    region_count = draw_region_count(jax.random.fold_in(key_list[20], 71), 0)
    projection = bell_draw(key_list[6], (C, D), C ** -0.5, 0.375, ((0, 2),))
    bn_gain = jnp.clip(jax.random.uniform(key_list[7], (D,), jnp.float32, 0.5, 1.5), 0.5, 1.5)
    bn_bias = jnp.clip(jax.random.uniform(key_list[8], (D,), jnp.float32, -1.0, 1.0), -1.0, 1.0)
    attn_in = bell_draw(key_list[9], (2, 3, D, D), (D // 2) ** -0.5, 0.3125, ((0, 2),))
    attn_bias = bell_draw(key_list[10], (2, 2, D), 0.5, 3.0, ((0, 2),), jnp.float32)
    attn_out = bell_draw(key_list[11], (2, D, D), (D // 16) ** -0.5, 0.875, ((0, 2),))
    attn_out_bias = bell_draw(key_list[12], (2, D), 0.5, 3.0, ((0, 2),), jnp.float32)
    ln_gain = jnp.clip(0.5 + 1.0 * jax.random.uniform(key_list[13], (2, 2, D), jnp.float32) ** steps_of(key_list[13], (2, 2, D), ((0, 2),), -0.2, 0.2), 0.5, 1.5)
    ln_bias = jnp.clip(jax.random.uniform(key_list[14], (2, 2, D), jnp.float32, -0.5, 0.5) * steps_of(key_list[14], (2, 2, D), ((0, 2),), -0.4, 0.0), -0.5, 0.5)
    w_up = bell_draw(key_list[15], (2, D, FF), D ** -0.5, 0.21875, ((0, 2),))
    b_up = bell_draw(key_list[16], (2, FF), 0.5, 3.0, ((0, 2),), jnp.float32)
    w_down = bell_draw(key_list[17], (2, FF, D), FF ** -0.5, 0.109375, ((0, 2),))
    b_down = bell_draw(key_list[18], (2, D), 0.5, 3.0, ((0, 2),), jnp.float32)
    cotangent = bell_draw(key_list[19], (TOKENS, D), 1.0, 6.0, ((0, 16),))
    return {"page_fine": page_fine, "page_coarse": page_coarse, "interp_fine": interp_fine, "interp_coarse": interp_coarse, "region_page": region_page, "region_count": region_count, "projection": projection, "bn_gain": bn_gain, "bn_bias": bn_bias, "attn_in": attn_in, "attn_bias": attn_bias, "attn_out": attn_out, "attn_out_bias": attn_out_bias, "ln_gain": ln_gain, "ln_bias": ln_bias, "w_up": w_up, "b_up": b_up, "w_down": w_down, "b_down": b_down, "cotangent": cotangent}


highest = lax.Precision.HIGHEST
norm_epsilon = 1e-05
masked_score = -1e+30

@jax.custom_vjp
def low(v):
    return lax.optimization_barrier(v.astype(jnp.bfloat16)).astype(jnp.float32)

@jax.custom_vjp
def low_back(v):
    return v

def low_keep(v):
    return (low(v), None)

def low_pass(kept, grad):
    return (grad,)

def back_keep(v):
    return (v, None)

def back_low(kept, grad):
    return (low(grad),)
low.defvjp(low_keep, low_pass)
low_back.defvjp(back_keep, back_low)

def rounded(value):
    return low_back(low(value))

def layer_norm(value, gain, shift):
    center = value - lax.optimization_barrier(jnp.mean(value, axis=-1, keepdims=True))
    spread = lax.optimization_barrier(jnp.mean(center * center, axis=-1, keepdims=True))
    return center * lax.rsqrt(spread + norm_epsilon) * gain + shift

def attend_group(inputs):
    query, key_rows, value_rows, live_rows = inputs
    groups, length, width = query.shape
    query_heads = query.reshape(groups, length, HEADS, HEAD)
    key_heads = key_rows.reshape(groups, length, HEADS, HEAD)
    value_heads = value_rows.reshape(groups, length, HEADS, HEAD)
    scores = jnp.einsum('gqhd,gkhd->ghqk', query_heads, key_heads, precision=highest) * 0.125
    scores = low_back(scores)
    scores = jnp.where(live_rows[:, None, None, :] > 0.5, scores, masked_score)
    top_score = lax.optimization_barrier(jnp.max(scores, axis=-1, keepdims=True))
    expos = jnp.exp(scores - top_score)
    weights = low(expos / lax.optimization_barrier(jnp.sum(expos, axis=-1, keepdims=True)))
    mixed = jnp.einsum('ghqk,gkhd->gqhd', weights, value_heads, precision=highest)
    return mixed.reshape(groups, length, width)

def encoder(layer_in, live_rows, layer, layer_params):
    attn_in, attn_bias, attn_out, attn_out_bias, ln_gain, ln_bias, w_up, b_up, w_down, b_down = layer_params
    triple = jnp.einsum('td,jde->jte', layer_in, attn_in[layer], precision=highest)
    query = rounded(triple[0] + attn_bias[layer, 0])
    key_rows = rounded(triple[1])
    value_rows = rounded(triple[2] + attn_bias[layer, 1])
    per_group = math.gcd(NSEQ, max(1, 4096 // SEQ))
    shape = (NSEQ // per_group, per_group, SEQ, D)
    mixed = lax.map(jax.checkpoint(attend_group), (query.reshape(shape), key_rows.reshape(shape), value_rows.reshape(shape), live_rows.reshape(NSEQ // per_group, per_group, SEQ)))
    mixed = rounded(mixed.reshape(TOKENS, D))
    branch = low_back(jnp.dot(mixed, attn_out[layer], preferred_element_type=jnp.float32, precision=highest) + attn_out_bias[layer])
    middle = layer_norm(layer_in + branch, ln_gain[layer, 0], ln_bias[layer, 0])
    before = low_back(jnp.dot(low(middle), w_up[layer], preferred_element_type=jnp.float32, precision=highest) + b_up[layer])
    active = low(jax.nn.gelu(before, approximate=False))
    feed = low_back(jnp.dot(active, w_down[layer], preferred_element_type=jnp.float32, precision=highest) + b_down[layer])
    return layer_norm(middle + feed, ln_gain[layer, 1], ln_bias[layer, 1])

def pool_pages(interp, onehot, maps):
    pixels = interp.shape[1]
    spread = (interp[:, None, :] * onehot[:, :, None]).reshape(N_DP, TOK_DEV, PAGES_DEV * pixels)
    tables = maps.reshape(N_DP, PAGES_DEV * pixels, C)
    return jnp.einsum('btx,bxc->btc', spread, tables, precision=highest).reshape(TOKENS, C)

def reference(page_fine, page_coarse, interp_fine, interp_coarse, region_page, region_count, projection, bn_gain, bn_bias, attn_in, attn_bias, attn_out, attn_out_bias, ln_gain, ln_bias, w_up, b_up, w_down, b_down, cotangent):
    row_ids = jnp.arange(TOKENS, dtype=jnp.int32)
    local_page = region_page - row_ids // TOK_DEV * PAGES_DEV
    onehot = (local_page[:, None] == jnp.arange(PAGES_DEV, dtype=jnp.int32)[None, :]).astype(jnp.float32)
    live_rows = (row_ids % SEQ < region_count[row_ids // SEQ]).astype(jnp.float32)
    fine_weights = interp_fine.astype(jnp.float32)
    coarse_weights = interp_coarse.astype(jnp.float32)

    def forward(maps_fine, maps_coarse, project, gain, shift, layer_params):
        pooled = rounded(pool_pages(fine_weights, onehot, maps_fine) + pool_pages(coarse_weights, onehot, maps_coarse))
        hidden = low_back(jnp.dot(pooled, project, preferred_element_type=jnp.float32, precision=highest))
        live_total = jnp.sum(live_rows)
        batch_mean = lax.optimization_barrier(jnp.sum(live_rows[:, None] * hidden, axis=0)) / live_total
        batch_var = lax.optimization_barrier(jnp.sum(live_rows[:, None] * hidden * hidden, axis=0)) / live_total - batch_mean * batch_mean
        first_in = rounded((hidden - batch_mean) * lax.rsqrt(batch_var + norm_epsilon) * gain + shift)
        first_out = encoder(first_in, live_rows, 0, layer_params)
        second_out = encoder(rounded(first_out), live_rows, 1, layer_params)
        return (second_out, (first_out, batch_mean, batch_var))
    layer_params = (attn_in.astype(jnp.float32), attn_bias, attn_out.astype(jnp.float32), attn_out_bias, ln_gain, ln_bias, w_up.astype(jnp.float32), b_up, w_down.astype(jnp.float32), b_down)
    second_out, pullback, extras = jax.vjp(forward, page_fine.astype(jnp.float32), page_coarse.astype(jnp.float32), projection.astype(jnp.float32), bn_gain, bn_bias, layer_params, has_aux=True)
    first_out, batch_mean, batch_var = extras
    d_fine, d_coarse, d_proj, d_gain, d_shift, d_layers = pullback(cotangent.astype(jnp.float32))
    return (jnp.stack([first_out, second_out]).astype(jnp.bfloat16), d_fine, d_coarse, d_proj, d_gain, d_shift, batch_mean, batch_var, d_layers[0], d_layers[1], d_layers[2], d_layers[3], d_layers[4], d_layers[5], d_layers[6], d_layers[7], d_layers[8], d_layers[9])
```

```python
import jax
import jax.numpy as jnp
from jax import lax
from jax.sharding import PartitionSpec as P

HEADS = 12
HEAD = 64

norm_epsilon = 1e-05
masked_score = -1e30


def exchanged(array, bit):
    length = lax.axis_size("dp")
    return lax.ppermute(array, "dp", [(i, i ^ (1 << bit)) for i in range(length)])


def dp_bit(bit):
    return (lax.axis_index("dp") >> bit) & 1


def halved(array, bit):
    half = array.shape[0] // 2
    mine = dp_bit(bit)
    keep = lax.dynamic_slice_in_dim(array, mine * half, half, 0)
    send = lax.dynamic_slice_in_dim(array, (1 - mine) * half, half, 0)
    got = exchanged(send, bit)
    return (keep.astype(jnp.float32) + got.astype(jnp.float32)).astype(jnp.bfloat16)


def doubled(array, bit):
    mine = dp_bit(bit)
    got = exchanged(array, bit)
    first = jnp.where(mine == 0, array, got)
    second = jnp.where(mine == 0, got, array)
    return jnp.concatenate([first, second], axis=0)


def bit_order(kind):
    bits = (lax.axis_size("dp") - 1).bit_length()
    order = list(range(bits))
    if kind == 1 and bits > 2:
        order = [0] + order[2:] + [1]
    return order


def summed_rows(array, kind):
    order = bit_order(kind)
    for bit in order:
        array = halved(array, bit)
    for bit in order[::-1]:
        array = doubled(array, bit)
    return array.astype(jnp.float32)


def summed_all(array):
    for bit in bit_order(0):
        array = array + exchanged(array, bit)
    return array


def layer_norm_parts(value):
    center = value - jnp.mean(value, axis=-1, keepdims=True)
    inv = lax.rsqrt(jnp.mean(center * center, axis=-1, keepdims=True) + norm_epsilon)
    return center * inv, inv


def norm_backward(d_out, normed, inv, gain):
    scaled = d_out * gain
    first = jnp.mean(scaled, axis=-1, keepdims=True)
    second = jnp.mean(scaled * normed, axis=-1, keepdims=True)
    return (scaled - first - normed * second) * inv


def split_heads(matrix):
    return matrix.reshape(matrix.shape[0], HEADS, HEAD)


def masked_scores(query, key_rows, live_seq):
    scores = (
        jnp.einsum(
            "qhd,khd->hqk",
            split_heads(query),
            split_heads(key_rows),
            preferred_element_type=jnp.float32,
        )
        * 0.125
    )
    return jnp.where(live_seq[None, None, :] > 0.5, scores, masked_score)


def attend_forward(query, key_rows, value_rows, live_seq):
    scores = masked_scores(query, key_rows, live_seq)
    top_score = jnp.max(scores, axis=-1, keepdims=True)
    expos = jnp.exp(scores - top_score)
    totals = jnp.sum(expos, axis=-1, keepdims=True)
    weights = (expos / totals).astype(jnp.bfloat16)
    mixed = jnp.einsum(
        "hqk,khd->qhd", weights, split_heads(value_rows), preferred_element_type=jnp.float32
    )
    return (mixed.reshape(query.shape).astype(jnp.bfloat16), top_score + jnp.log(totals))


def attend_backward(query, key_rows, value_rows, live_seq, log_total, d_mixed):
    scores = masked_scores(query, key_rows, live_seq)
    weights = jnp.exp(scores - log_total)
    d_heads = split_heads(d_mixed)
    d_weights = jnp.einsum(
        "qhd,khd->hqk", d_heads, split_heads(value_rows), preferred_element_type=jnp.float32
    )
    d_values = jnp.einsum(
        "hqk,qhd->khd", weights.astype(jnp.bfloat16), d_heads, preferred_element_type=jnp.float32
    )
    inner = jnp.sum(weights * d_weights, axis=-1, keepdims=True)
    d_scores = (weights * (d_weights - inner)).astype(jnp.bfloat16)
    d_query = (
        jnp.einsum(
            "hqk,khd->qhd", d_scores, split_heads(key_rows), preferred_element_type=jnp.float32
        )
        * 0.125
    )
    d_keys = (
        jnp.einsum("hqk,qhd->khd", d_scores, split_heads(query), preferred_element_type=jnp.float32)
        * 0.125
    )
    shape = query.shape
    return jnp.concatenate(
        [d_query.reshape(shape), d_keys.reshape(shape), d_values.reshape(shape)], axis=1
    ).astype(jnp.bfloat16)


def dot(left, right):
    return jnp.dot(left, right, preferred_element_type=jnp.float32)


def dot_right_t(left, right):
    return lax.dot_general(
        left, right, (((1,), (1,)), ((), ())), preferred_element_type=jnp.float32
    )


def dot_left_t(left, right):
    return lax.dot_general(
        left, right, (((0,), (0,)), ((), ())), preferred_element_type=jnp.float32
    )


def layer_forward(layer_in, live_seq, params):
    attn_in, attn_bias, attn_out, attn_out_bias, ln_gain, ln_bias, w_up, b_up, w_down, b_down = (
        params
    )
    query = (dot(layer_in, attn_in[0]) + attn_bias[0]).astype(jnp.bfloat16)
    key_rows = dot(layer_in, attn_in[1]).astype(jnp.bfloat16)
    value_rows = (dot(layer_in, attn_in[2]) + attn_bias[1]).astype(jnp.bfloat16)
    mixed, log_total = attend_forward(query, key_rows, value_rows, live_seq)
    first_sum = layer_in.astype(jnp.float32) + (dot(mixed, attn_out) + attn_out_bias)
    first_normed, first_inv = layer_norm_parts(first_sum)
    middle = first_normed * ln_gain[0] + ln_bias[0]
    middle_low = middle.astype(jnp.bfloat16)
    before = dot(middle_low, w_up) + b_up
    cumulative = 0.5 * (1.0 + lax.erf(before * 0.7071067811865476))
    active = (before * cumulative).astype(jnp.bfloat16)
    slope = (cumulative + before * 0.3989422804014327 * jnp.exp(-0.5 * before * before)).astype(
        jnp.bfloat16
    )
    second_sum = middle + (dot(active, w_down) + b_down)
    second_normed, second_inv = layer_norm_parts(second_sum)
    result = (second_normed * ln_gain[1] + ln_bias[1]).astype(jnp.bfloat16)
    kept = dict(
        layer_in=layer_in,
        live_seq=live_seq,
        query=query,
        key_rows=key_rows,
        value_rows=value_rows,
        log_total=log_total,
        mixed=mixed,
        first_normed=first_normed,
        first_inv=first_inv,
        middle_low=middle_low,
        active=active,
        slope=slope,
        second_normed=second_normed,
        second_inv=second_inv,
    )
    return result, kept


def layer_backward(d_result, kept, params):
    attn_in, attn_bias, attn_out, attn_out_bias, ln_gain, ln_bias, w_up, b_up, w_down, b_down = (
        params
    )
    d_second = norm_backward(d_result, kept["second_normed"], kept["second_inv"], ln_gain[1])
    d_gain_two = jnp.sum(d_result * kept["second_normed"], axis=0)
    d_shift_two = jnp.sum(d_result, axis=0)
    d_feed = d_second.astype(jnp.bfloat16)
    d_b_down = jnp.sum(d_feed.astype(jnp.float32), axis=0)
    d_before = (kept["slope"].astype(jnp.float32) * dot_right_t(d_feed, w_down)).astype(
        jnp.bfloat16
    )
    d_b_up = jnp.sum(d_before.astype(jnp.float32), axis=0)
    d_middle = d_second + dot_right_t(d_before, w_up)
    d_first = norm_backward(d_middle, kept["first_normed"], kept["first_inv"], ln_gain[0])
    d_gain_one = jnp.sum(d_middle * kept["first_normed"], axis=0)
    d_shift_one = jnp.sum(d_middle, axis=0)
    d_branch = d_first.astype(jnp.bfloat16)
    d_out_bias = jnp.sum(d_branch.astype(jnp.float32), axis=0)
    d_mixed = dot_right_t(d_branch, attn_out).astype(jnp.bfloat16)
    d_triple = attend_backward(
        kept["query"],
        kept["key_rows"],
        kept["value_rows"],
        kept["live_seq"],
        kept["log_total"],
        d_mixed,
    )
    width = d_mixed.shape[1]
    d_bias = jnp.sum(d_triple.astype(jnp.float32), axis=0)
    d_layer_in = d_first
    for part in range(3):
        d_layer_in = d_layer_in + dot_right_t(
            d_triple[:, part * width : (part + 1) * width], attn_in[part]
        )
    small = jnp.concatenate(
        [
            d_bias[:width],
            d_bias[2 * width :],
            d_out_bias,
            d_gain_one,
            d_gain_two,
            d_shift_one,
            d_shift_two,
            d_b_up,
            d_b_down,
        ]
    )
    grads = dict(d_feed=d_feed, d_before=d_before, d_branch=d_branch, d_triple=d_triple)
    return d_layer_in.astype(jnp.bfloat16), grads, small


def local(
    page_fine,
    page_coarse,
    interp_fine,
    interp_coarse,
    region_page,
    region_count,
    projection,
    bn_gain,
    bn_bias,
    attn_in,
    attn_bias,
    attn_out,
    attn_out_bias,
    ln_gain,
    ln_bias,
    w_up,
    b_up,
    w_down,
    b_down,
    cotangent,
):
    row_count, width = cotangent.shape
    page_count = page_fine.shape[0]
    channel_half = page_fine.shape[2]
    micro_count = region_count.shape[0]
    seq_length = row_count // micro_count
    hidden_units = w_up.shape[2]
    section = lax.axis_index("section")
    data_index = lax.axis_index("dp")
    lower = section == 0
    params = (
        attn_in[0],
        attn_bias[0],
        attn_out[0],
        attn_out_bias[0],
        ln_gain[0],
        ln_bias[0],
        w_up[0],
        b_up[0],
        w_down[0],
        b_down[0],
    )

    def both_sections(array, axis):
        other = lax.ppermute(array, "section", [(0, 1), (1, 0)])
        return jnp.concatenate(
            [jnp.where(lower, array, other), jnp.where(lower, other, array)], axis=axis
        )

    def upward(array):
        return lax.ppermute(array, "section", [(0, 1)])

    def downward(array):
        return lax.ppermute(array, "section", [(1, 0)])

    whole_projection = both_sections(projection, 0)
    positions = lax.broadcasted_iota(jnp.int32, (micro_count, seq_length), 1)
    live_mask = (positions < region_count[:, None]).astype(jnp.float32)
    live_rows = live_mask.reshape(row_count, 1)
    local_page = region_page - data_index * page_count
    page_slots = lax.broadcasted_iota(jnp.int32, (row_count, page_count), 1)
    onehot = (local_page[:, None] == page_slots).astype(jnp.bfloat16)
    spread = jnp.concatenate(
        [
            (onehot[:, :, None] * interp_fine[:, None, :]).reshape(row_count, -1),
            (onehot[:, :, None] * interp_coarse[:, None, :]).reshape(row_count, -1),
        ],
        axis=1,
    )
    tables = jnp.concatenate(
        [page_fine.reshape(-1, channel_half), page_coarse.reshape(-1, channel_half)], axis=0
    )
    pooled = both_sections(dot(spread, tables).astype(jnp.bfloat16), 1)
    hidden = dot(pooled, whole_projection)
    weighted = live_rows * hidden
    moments = summed_all(
        jnp.stack(
            [
                jnp.sum(weighted, axis=0),
                jnp.sum(weighted * hidden, axis=0),
                jnp.broadcast_to(jnp.sum(live_rows), (width,)),
            ]
        )
    )
    live_total = moments[2, 0]
    bn_mean = moments[0] / live_total
    bn_var = moments[1] / live_total - bn_mean * bn_mean
    inv_std = lax.rsqrt(bn_var + norm_epsilon)
    centered = (hidden - bn_mean) * inv_std
    first_in = (centered * bn_gain + bn_bias).astype(jnp.bfloat16)

    def seq_of(array, micro):
        return array[micro * seq_length : (micro + 1) * seq_length]

    results, kept = [], []
    received = None
    for tick in range(micro_count + 1):
        if tick == 0:
            layer_in, live_seq = seq_of(first_in, 0), live_mask[0]
        elif tick == micro_count:
            layer_in, live_seq = received, live_mask[micro_count - 1]
        else:
            layer_in = jnp.where(lower, seq_of(first_in, tick), received)
            live_seq = jnp.where(lower, live_mask[tick], live_mask[tick - 1])
        result, saved = layer_forward(layer_in, live_seq, params)
        if tick < micro_count:
            received = upward(result)
        results.append(result)
        kept.append(saved)
    own_results = jnp.concatenate(
        [jnp.where(lower, results[m], results[m + 1]) for m in range(micro_count)], axis=0
    )[None]

    grads, smalls, sent = [], [], []
    received = None
    for tick in range(micro_count + 1):
        if tick == 0:
            saved, d_result = kept[1], seq_of(cotangent, 0)
        elif tick == micro_count:
            saved, d_result = kept[micro_count - 1], received
        else:
            saved = jax.tree.map(
                lambda one, two: jnp.where(lower, one, two), kept[tick - 1], kept[tick + 1]
            )
            d_result = jnp.where(lower, received, seq_of(cotangent, tick))
        d_layer_in, grad, small = layer_backward(d_result.astype(jnp.float32), saved, params)
        if tick < micro_count:
            received = downward(d_layer_in)
        grads.append(grad)
        smalls.append(small)
        sent.append(d_layer_in)

    def kept_rows(name):
        return jnp.concatenate(
            [jnp.where(lower, kept[m][name], kept[m + 1][name]) for m in range(micro_count)], axis=0
        )

    def grad_rows(name):
        return jnp.concatenate(
            [jnp.where(lower, grads[m + 1][name], grads[m][name]) for m in range(micro_count)],
            axis=0,
        )

    small_sum = sum(jnp.where(lower, smalls[m + 1], smalls[m]) for m in range(micro_count))

    d_normed = jnp.concatenate(sent[1:], axis=0).astype(jnp.float32)
    bn_sums = jnp.stack([jnp.sum(d_normed, axis=0), jnp.sum(d_normed * centered, axis=0)])
    small_count = small_sum.shape[0]
    vector_sums = summed_all(jnp.concatenate([bn_sums.reshape(-1), small_sum]))
    bn_sums = vector_sums[: 2 * width].reshape(2, width)
    small_total = vector_sums[2 * width :]
    d_hidden = (
        inv_std
        * bn_gain
        * (d_normed - live_rows * (bn_sums[0] + centered * bn_sums[1]) / live_total)
    ).astype(jnp.bfloat16)
    proj_sum = dot_left_t(pooled, d_hidden).astype(jnp.bfloat16)
    d_pooled = dot_right_t(d_hidden, whole_projection).astype(jnp.bfloat16)
    up_sums = upward(bn_sums)
    up_proj = upward(proj_sum[channel_half:])
    up_pooled = upward(d_pooled[:, channel_half:])
    bn_sums = jnp.where(lower, bn_sums, up_sums)
    proj_sum = jnp.where(lower, proj_sum[:channel_half], up_proj)
    d_pooled = jnp.where(lower, d_pooled[:, :channel_half], up_pooled)
    map_grad = dot_left_t(spread, d_pooled)
    fine_size = page_count * interp_fine.shape[1]
    fine_grad = map_grad[:fine_size].reshape(page_fine.shape)
    coarse_grad = map_grad[fine_size:].reshape(page_coarse.shape)

    active, d_feed = kept_rows("active"), grad_rows("d_feed")
    middle_low, d_before = kept_rows("middle_low"), grad_rows("d_before")
    mixed, d_branch = kept_rows("mixed"), grad_rows("d_branch")
    layer_in, d_triple = kept_rows("layer_in"), grad_rows("d_triple")
    half = hidden_units // 2
    down = [
        summed_rows(dot_left_t(active[:, j * half : (j + 1) * half], d_feed).astype(jnp.bfloat16), j)
        for j in range(2)
    ]
    up = [
        summed_rows(
            dot_left_t(middle_low, d_before[:, j * half : (j + 1) * half]).astype(jnp.bfloat16), 0
        )
        for j in range(2)
    ]
    out_grad = summed_rows(dot_left_t(mixed, d_branch).astype(jnp.bfloat16), 0)
    in_grad = [
        summed_rows(
            dot_left_t(layer_in, d_triple[:, j * width : (j + 1) * width]).astype(jnp.bfloat16), 0
        )
        for j in range(3)
    ]
    proj_total = summed_all(proj_sum).astype(jnp.float32)

    pieces = [
        small_total[j * width : (j + 1) * width] for j in range(7)
    ]
    b_up_total = small_total[7 * width : 7 * width + hidden_units]
    b_down_total = small_total[7 * width + hidden_units :]
    return (
        own_results,
        fine_grad,
        coarse_grad,
        proj_total,
        bn_sums[1],
        bn_sums[0],
        bn_mean,
        bn_var,
        jnp.stack(in_grad)[None],
        jnp.stack(pieces[0:2])[None],
        out_grad[None],
        pieces[2][None],
        jnp.stack(pieces[3:5])[None],
        jnp.stack(pieces[5:7])[None],
        jnp.concatenate(up, axis=1)[None],
        b_up_total[None],
        jnp.concatenate(down, axis=0)[None],
        b_down_total[None],
    )


def solution(mesh):
    return jax.shard_map(
        local,
        mesh=mesh,
        in_specs=(
            P("dp", None, "section"),
            P("dp", None, "section"),
            P("dp", None),
            P("dp", None),
            P("dp"),
            P("dp"),
            P("section", None),
            P(),
            P(),
            P("section", None, None, None),
            P("section", None, None),
            P("section", None, None),
            P("section", None),
            P("section", None, None),
            P("section", None, None),
            P("section", None, None),
            P("section", None),
            P("section", None, None),
            P("section", None),
            P("dp", None),
        ),
        out_specs=(
            P("section", "dp", None),
            P("dp", None, "section"),
            P("dp", None, "section"),
            P("section", None),
            P(),
            P(),
            P(),
            P(),
            P("section", None, None, None),
            P("section", None, None),
            P("section", None, None),
            P("section", None),
            P("section", None, None),
            P("section", None, None),
            P("section", None, None),
            P("section", None),
            P("section", None, None),
            P("section", None),
        ),
        check_vma=False,
    )
```
